32 devices in a mesh: grp: 2 (over x), sub: 16 (over z, y, core).
Axes of the slice: x: 2, y: 2, z: 4, core: 2. Of those that a mesh axis runs over, the one named last changes fastest.
Arguments:
- load_cases: float32 [36864, 128], P(('grp', 'sub')), may hold values from -6 to 6
- schur_matrix: float32 [36864, 1152], P(('grp', 'sub')), may hold values from -0.0017361111 to 16, as said below
- local_inverse: float32 [36864, 1152], P(('grp', 'sub')), may hold values from -0.00021701389 to 2, as said below
- coarse_basis: float32 [1024, 1152], P(('grp', 'sub')), may hold values from -0.375 to 0.375
- group_inverse: float32 [1024, 512], P(('grp', 'sub')), may hold values from -0.0009765625 to 4, as said below
- group_modes: float32 [1024, 32], P(('grp', 'sub')), may hold values from -0.375 to 0.375
- top_inverse: float32 [64, 64], replicated, may hold values from -0.0078125 to 4, as said below
- face_map: int32 [32, 1152], P(('grp', 'sub')), may hold values from 0 to 1151, each once within a row
- spectrum: float32 [2], replicated, may hold values from 0.1 to 6, as said below
Outputs:
- solution: float32 [36864, 128], P(('grp', 'sub'))
- residual: float32 [36864, 128], P(('grp', 'sub'))
The draws below stay inside these ranges and needn't reach their ends.
Inputs may be any that keep to these rules, and one draw needn't show every extreme that they name: `face_map`: each row is a permutation of 0 to 1151. `schur_matrix`: each subdomain's 1152 x 1152 block is symmetric positive definite. `local_inverse`: each subdomain's 1152 x 1152 block is symmetric positive definite. `group_inverse`: each group's 512 x 512 block is symmetric positive definite. `top_inverse`: symmetric positive definite. spectrum[0] < spectrum[1].
All inputs are finite; a program needn't handle non-finite values.
Results may differ from the reference program's by a relative error of at most 0.00011.
Values sent between devices are 32-bit elements; how exact they have to be, the bound alone decides.
A program may use at most 64 MiB of HBM per device.

```python
import math
import jax
import jax.numpy as jnp
from jax import lax

FACE = 288
ORDER = 1152
MODES = 32
CASES = 128
ITERS = 3
DOMAINS = 32
COARSE = 512
APEX_DOFS = 64
N_GRP = 2
N_SUB = 16


def dominant(key, number, order, spread, diag_low, diag_high):
    first_key, second_key = jax.random.split(key)
    raw = jax.random.uniform(first_key, (number, order, order), jnp.float32, -1.0, 1.0)
    offdiag = (raw + jnp.swapaxes(raw, 1, 2)) * (0.5 * spread / order)
    levels = jnp.exp(jax.random.uniform(second_key, (number, order, 1), jnp.float32, math.log(diag_low), math.log(diag_high)))
    diagonal_mask = lax.broadcasted_iota(jnp.int32, (order, order), 0) == lax.broadcasted_iota(jnp.int32, (order, order), 1)
    return jnp.where(diagonal_mask[None], levels, offdiag)


def draw_schur_matrix(key, part):
    blocks = dominant(key, DOMAINS, ORDER, 2.0, 2.0, 4.0)
    return blocks.reshape(DOMAINS * ORDER, ORDER)


def draw_local_inverse(key, part):
    blocks = dominant(key, DOMAINS, ORDER, 0.25, 0.25, 0.5)
    return blocks.reshape(DOMAINS * ORDER, ORDER)


def draw_group_inverse(key, part):
    groups = APEX_DOFS // MODES
    blocks = dominant(key, groups, COARSE, 0.5, 0.5, 1.0)
    return blocks.reshape(groups * COARSE, COARSE)


def draw_top_inverse(key, part):
    blocks = dominant(key, 1, APEX_DOFS, 0.5, 0.5, 1.0)
    return blocks[0]


def draw_spectrum(key, part):
    first_key, second_key = jax.random.split(key)
    lower = jax.random.uniform(first_key, (), jnp.float32, 0.2, 0.4)
    upper = jax.random.uniform(second_key, (), jnp.float32, 2.5, 4.0)
    return jnp.stack([lower, upper])


def shard_levels(stream_key, shape, cuts, low, top_value):
    loudness, own = 1.0, jax.random.fold_in(stream_key, 6)
    for dim, parts in cuts:
        draws = jnp.exp(jax.random.uniform(jax.random.fold_in(own, dim), (parts,), jnp.float32, low / len(cuts), top_value / len(cuts)))
        loudness = loudness * jnp.repeat(draws, shape[dim] // parts).reshape([-1 if axis == dim else 1 for axis in range(len(shape))])
    return loudness


def normal_values(rng, dims, deviation, limit, shards=(), held_as=jnp.bfloat16):
    level = shard_levels(rng, dims, shards, -0.22, 0.18) if shards else 1.0
    values = jax.random.normal(rng, dims, jnp.float32) * deviation * level
    return jnp.minimum(jnp.maximum(values, -limit), limit).astype(held_as)


def setup_inputs(seed: int = 0) -> dict:
    key_of = jax.random.split(jax.random.key(seed), 10)
    load_cases = normal_values(key_of[0], (DOMAINS * ORDER, CASES), 1.0, 6.0, ((0, 32),), jnp.float32)
    schur_matrix = draw_schur_matrix(jax.random.fold_in(key_of[9], 71), 0)
    local_inverse = draw_local_inverse(jax.random.fold_in(key_of[9], 71), 0)
    coarse_basis = normal_values(key_of[3], (DOMAINS * MODES, ORDER), (ORDER // 4) ** -0.5, 0.375, ((0, 32),), jnp.float32)
    group_inverse = draw_group_inverse(jax.random.fold_in(key_of[9], 71), 0)
    group_modes = normal_values(key_of[5], (DOMAINS * MODES, MODES), (8 * MODES) ** -0.5, 0.375, ((0, 32),), jnp.float32)
    top_inverse = draw_top_inverse(jax.random.fold_in(key_of[9], 71), 0)
    face_map = jax.vmap(lambda own: jax.random.permutation(own, ORDER))(jax.random.split(key_of[7], DOMAINS)).reshape((DOMAINS, ORDER)).astype(jnp.int32)
    spectrum = draw_spectrum(jax.random.fold_in(key_of[9], 71), 0)
    return dict(load_cases=load_cases, schur_matrix=schur_matrix, local_inverse=local_inverse, coarse_basis=coarse_basis, group_inverse=group_inverse, group_modes=group_modes, top_inverse=top_inverse, face_map=face_map, spectrum=spectrum)


def assemble(values, face_map, inverse_map):
    columns = values.shape[-1]
    face_rows = jnp.take_along_axis(values, face_map[:, :, None], axis=1).reshape(N_GRP, N_SUB, 4, FACE, columns)
    zero_grp = jnp.zeros_like(face_rows[:1, :, 0])
    zero_sub = jnp.zeros_like(face_rows[:, :1, 0])
    from_low = jnp.concatenate([zero_grp, face_rows[:-1, :, 1]], axis=0)
    from_high = jnp.concatenate([face_rows[1:, :, 0], zero_grp], axis=0)
    from_left = jnp.concatenate([zero_sub, face_rows[:, :-1, 3]], axis=1)
    from_right = jnp.concatenate([face_rows[:, 1:, 2], zero_sub], axis=1)
    received = jnp.stack([from_low, from_high, from_left, from_right], axis=2).reshape(DOMAINS, ORDER, columns)
    return values + jnp.take_along_axis(received, inverse_map[:, :, None], axis=1)


def reference(load_cases, schur_matrix, local_inverse, coarse_basis, group_inverse, group_modes, top_inverse, face_map, spectrum):
    largest_bound = lax.Precision.HIGHEST
    inverse_map = jnp.argsort(face_map, axis=1).astype(jnp.int32)
    grp_ids = jnp.arange(N_GRP)[:, None]
    sub_ids = jnp.arange(N_SUB)[None, :]
    has_side = jnp.stack([jnp.broadcast_to(grp_ids > 0, (N_GRP, N_SUB)),
                          jnp.broadcast_to(grp_ids < N_GRP - 1, (N_GRP, N_SUB)),
                          jnp.broadcast_to(sub_ids > 0, (N_GRP, N_SUB)),
                          jnp.broadcast_to(sub_ids < N_SUB - 1, (N_GRP, N_SUB))], axis=-1)
    face_weight = jnp.where(has_side, 0.5, 1.0).astype(jnp.float32).reshape(DOMAINS, 4)
    face_weight = jnp.repeat(face_weight, FACE, axis=1)
    weight = jnp.take_along_axis(face_weight, inverse_map, axis=1)[:, :, None]

    schur_blocks = schur_matrix.reshape(DOMAINS, ORDER, ORDER)
    inverse_blocks = local_inverse.reshape(DOMAINS, ORDER, ORDER)
    basis = coarse_basis.reshape(DOMAINS, MODES, ORDER)
    group_blocks = group_inverse.reshape(N_GRP, COARSE, COARSE)
    cluster_basis = group_modes.reshape(N_GRP, COARSE, MODES)

    def precondition(residual):
        weighted = weight * residual
        local_part = jnp.einsum('dab,dbr->dar', inverse_blocks, weighted, precision=largest_bound)
        coarse = jnp.einsum('dma,dar->dmr', basis, weighted, precision=largest_bound)
        piled_vectors = coarse.reshape(N_GRP, COARSE, -1)
        cluster_portion = jnp.einsum('gab,gbr->gar', group_blocks, piled_vectors, precision=largest_bound)
        apex_input = jnp.einsum('kli,klp->kip', cluster_basis, piled_vectors, precision=largest_bound).reshape(APEX_DOFS, -1)
        apex_output = jnp.dot(top_inverse, apex_input, precision=largest_bound).reshape(N_GRP, MODES, -1)
        update_term = cluster_portion + jnp.einsum('usl,ule->use', cluster_basis, apex_output, precision=largest_bound)
        update_term = update_term.reshape(DOMAINS, MODES, -1)
        summed = local_part + jnp.einsum('dma,dmr->dar', basis, update_term, precision=largest_bound)
        return assemble(weight * summed, face_map, inverse_map)

    centre = 0.5 * (spectrum[0] + spectrum[1])
    half_width = 0.5 * (spectrum[1] - spectrum[0])
    residual = assemble(load_cases.reshape(DOMAINS, ORDER, CASES), face_map, inverse_map)
    direction = precondition(residual) / centre
    rho_now = half_width / centre
    solution = jnp.zeros_like(residual)
    for turn_index in range(ITERS):
        solution = solution + direction
        applied = jnp.einsum('dab,dbr->dar', schur_blocks, direction, precision=largest_bound)
        residual = residual - assemble(applied, face_map, inverse_map)
        if turn_index + 1 < ITERS:
            rho_next = 1.0 / (2.0 * centre / half_width - rho_now)
            direction = rho_next * rho_now * direction + (2.0 * rho_next / half_width) * precondition(residual)
            rho_now = rho_next
    return solution.reshape(DOMAINS * ORDER, CASES), residual.reshape(DOMAINS * ORDER, CASES)
```

```python
import functools

import jax
import jax.numpy as jnp
from jax import lax
from jax.experimental import pallas as pl
from jax.experimental.pallas import tpu as pltpu
from jax.sharding import PartitionSpec as P

ITERS = 3
F32 = jnp.float32
BF16 = jnp.bfloat16
MESH = pl.DeviceIdType.MESH
FIRST = (((0,), (0,)), ((), ()))
LAST = (((1,), (1,)), ((), ()))


def dot(a, b):
    return jnp.dot(a, b, preferred_element_type=F32)


def dot_first(a, b):
    return lax.dot_general(a, b, FIRST, preferred_element_type=F32)


def dot_last(a, b):
    return lax.dot_general(a, b, LAST, preferred_element_type=F32)


def exact_dot(a, b):
    return jnp.dot(a, b, precision=lax.Precision.HIGHEST, preferred_element_type=F32)


def split(v):
    high = v.astype(BF16)
    low = (v - high.astype(F32)).astype(BF16)
    return high, low


def kernel(
    n_grp, n_sub, n_low,
    load, schur, linv, basis, ginv, gm, top, fmap, spec,
    sol_out, res_out,
    stage_l, stage_a, stage_s, a2, s2, sp2, perm, map_column, b2, bcat, x2, xl2, z2, xcat, direction, residual,
    sendb, recvb, b_out, b_in, line_out, line_in, plane_modes, t2, plane, c2, part_out, part_in, x_out, x_in,
    load_sem, face_send, face_recv, p_send, p_recv, z_send, z_recv, n_send, n_recv,
):
    order, columns = sol_out.shape
    face = order // 4
    modes = basis.shape[0]
    n_high = n_sub // n_low
    n_plane = n_grp * n_low
    row_modes = n_low * modes
    tile = 128
    g = lax.axis_index("grp")
    j = lax.axis_index("sub")
    high, low = j // n_low, j % n_low
    mine = g * n_low + low

    first = jnp.where(g == 0, 1, 0)
    third = jnp.where(j == 0, 1, 0)
    face_of = [first, 1 - first, 2 + third, 3 - third]
    present = [True, jnp.logical_and(g > 0, g < n_grp - 1), True, jnp.logical_and(j > 0, j < n_sub - 1)]
    peer = [{"grp": jnp.where(g == 0, 1, g - 1)}, {"grp": g + 1}, {"sub": jnp.where(j == 0, 1, j - 1)}, {"sub": j + 1}]
    landing = [jnp.where(g >= 2, 1, 0) if n_grp > 2 else 0, 0, jnp.where(j >= 2, 3, 2) if n_sub > 2 else 2, 2]
    shared = [0, 2] + ([1] if n_grp > 2 else []) + ([3] if n_sub > 2 else [])
    weight = [0.5, jnp.where(present[1], 0.5, 1.0).astype(F32) if n_grp > 2 else 1.0,
              0.5, jnp.where(present[3], 0.5, 1.0).astype(F32) if n_sub > 2 else 1.0]

    def guard(f, action):
        if f in (0, 2):
            action()
        else:
            pl.when(present[f])(action)

    load_l = pltpu.make_async_copy(load, stage_l, load_sem.at[0])
    load_a = pltpu.make_async_copy(linv, stage_a, load_sem.at[1])
    load_s = pltpu.make_async_copy(schur, stage_s, load_sem.at[2])
    load_l.start()
    load_a.start()
    load_s.start()

    def plane_peer(k):
        q = lax.rem(mine + k, n_plane)
        return {"grp": q // n_low, "sub": high * n_low + lax.rem(q, n_low)}

    def line_at(k):
        return lax.rem(high + k, n_high)

    def line_peer(k):
        return {"sub": line_at(k) * n_low + low}

    barrier = pltpu.get_barrier_semaphore()
    for k in range(1, n_plane):
        pl.semaphore_signal(barrier, inc=1, device_id=plane_peer(k), device_id_type=MESH)
    for k in range(1, n_high):
        pl.semaphore_signal(barrier, inc=1, device_id=line_peer(k), device_id_type=MESH)
    for f in (2, 3):
        if f in shared:
            guard(f, lambda: pl.semaphore_signal(barrier, inc=1, device_id=peer[f], device_id_type=MESH))
    expected = n_plane - 1 + n_high - 1 + 1
    if 3 in shared:
        expected = expected + jnp.where(present[3], 1, 0)

    def remote(src, dst, send, recv, device):
        return pltpu.make_async_remote_copy(
            src_ref=src, dst_ref=dst, send_sem=send, recv_sem=recv, device_id=device, device_id_type=MESH)

    def face_copy(r, f):
        return remote(sendb.at[r, f], recvb.at[r, landing[f]], face_send.at[r, f], face_recv.at[r, landing[f]], peer[f])

    def face_arrival(r, f):
        return remote(sendb.at[r, f], recvb.at[r, f], face_send.at[r, f], face_recv.at[r, f], peer[f])

    def basis_copy(f):
        return remote(b_out.at[f], b_in.at[landing[f]], n_send.at[0, f], n_recv.at[0, landing[f]], peer[f])

    def basis_arrival(f):
        return remote(b_out.at[f], b_in.at[f], n_send.at[0, f], n_recv.at[0, f], peer[f])

    def coarse_copy(c, f):
        return remote(x_out.at[c], x_in.at[c, landing[f]], n_send.at[1 + c, f], n_recv.at[1 + c, landing[f]], peer[f])

    def coarse_arrival(c, f):
        return remote(x_out.at[c], x_in.at[c, f], n_send.at[1 + c, f], n_recv.at[1 + c, f], peer[f])

    def modes_copy(k, slot):
        return remote(plane_modes.at[slot], plane_modes.at[slot], p_send.at[0, k], p_recv.at[0, k], plane_peer(k))

    def plane_copy(c, k, slot):
        return remote(plane.at[c, slot], plane.at[c, slot], p_send.at[1 + c, k], p_recv.at[1 + c, k], plane_peer(k))

    def from_plane(k):
        return lax.rem(mine + n_plane - k, n_plane)

    def line_copy(k, slot):
        return remote(line_out.at[line_at(k)], line_in.at[slot], z_send.at[0, k], z_recv.at[0, k], line_peer(k))

    def part_copy(c, k):
        return remote(part_out.at[c, line_at(k)], part_in.at[c, k], z_send.at[1 + c, k], z_recv.at[1 + c, k], line_peer(k))

    def from_line(k):
        return lax.rem(high + n_high - k, n_high)

    def send_face(r, f):
        if f in shared:
            guard(f, lambda: face_copy(r, f).start())

    def await_faces(r):
        for f in reversed(shared):
            guard(f, lambda: face_arrival(r, f).wait_recv())

    def received(r, f):
        if f not in shared:
            return None
        value = recvb[r, f]
        return value if f in (0, 2) else jnp.where(present[f], value, 0.0)

    def assembled(r, f):
        value = received(r, f)
        return sendb[r, f] if value is None else sendb[r, f] + value

    def halves(out):
        return out[:, :columns] + out[:, columns:]

    def put(ref, rows, value):
        upper, lower = split(value)
        ref[rows, :columns] = upper
        ref[rows, columns:] = lower

    def slot_rows(f):
        return slice(f * face, (f + 1) * face)

    map_row = fmap[...].astype(F32)
    map_column[...] = jnp.broadcast_to(map_row, (tile, order)).T
    lanes = lax.broadcasted_iota(jnp.int32, (face, tile), 1).astype(F32)
    for f in range(4):
        own = map_column[pl.ds(pl.multiple_of(face_of[f] * face, 16), face), :]
        for t in range(order // tile):
            perm[slot_rows(f), t * tile:(t + 1) * tile] = jnp.where(own == lanes + float(t * tile), 1.0, 0.0).astype(BF16)

    width = plane_modes.shape[2]
    row = lax.broadcasted_iota(jnp.int32, (modes, width), 0)
    lane = lax.broadcasted_iota(jnp.int32, (modes, width), 1)
    plane_modes[mine] = exact_dot(gm[...], jnp.where(lane == row + g * modes, 1.0, 0.0).astype(F32))
    own_modes = jnp.concatenate([gm[...], jnp.zeros((modes, tile - modes), F32)], axis=1)
    for h in range(n_high):
        line_out[h, :, :row_modes] = ginv[:, h * row_modes:(h + 1) * row_modes]
        line_out[h, :, row_modes:] = own_modes

    pl.semaphore_wait(barrier, expected)

    for k in range(1, n_high):
        line_copy(k, high).start()
    for k in range(1, n_plane):
        modes_copy(k, mine).start()

    load_l.wait()
    for i in range(4):
        put(z2, slot_rows(i), stage_l[slot_rows(i), :])
    for f in (0, 2, 3, 1):
        sendb[0, f] = halves(dot(perm[slot_rows(f), :], z2[...]))
        send_face(0, f)

    upper, lower = split(basis[...])
    both = jnp.concatenate([upper, lower], axis=0)
    b2[...] = dot_last(both, perm[...]).astype(BF16)
    for f in range(4):
        moved = dot_last(both, perm[slot_rows(f), :])
        b_out[f] = jnp.zeros(b_out.shape[1:], F32)
        b_out[f, :, :face] = moved[:modes] + moved[modes:]
        if f in shared:
            guard(f, lambda: basis_copy(f).start())
        upper, lower = split(b_out[f])
        bcat[f, :modes, :] = upper
        bcat[f, modes:2 * modes, :] = lower

    def split_matrix(stage, matrix):
        def chunk(i, carry):
            rows = pl.ds(pl.multiple_of(i * tile, tile), tile)
            upper, lower = split(stage[rows, :])
            matrix[rows, :order] = upper
            matrix[rows, order:] = lower
            return carry
        lax.fori_loop(0, order // tile, chunk, 0)

    def permute_schur(start, stop):
        for i in range(start, stop):
            lanes = slice(2 * i * tile, 2 * (i + 1) * tile)
            sp2[:, lanes] = dot(perm[...], s2[:, lanes]).astype(BF16)
    blocks = order // tile

    load_a.wait()
    split_matrix(stage_a, a2)
    load_s.wait()
    split_matrix(stage_s, s2)

    line_in[high] = line_out[high]
    for k in range(1, n_high):
        line_copy(k, from_line(k)).wait_recv()
    for k in range(1, n_plane):
        modes_copy(k, from_plane(k)).wait_recv()
    lines = line_in[...].reshape(n_high * modes, row_modes + tile)
    top_rows = top[pl.ds(pl.multiple_of(g * modes, modes), modes), :]
    through = exact_dot(lines[:, row_modes:row_modes + modes], top_rows)
    sources = plane_modes[...].reshape(n_plane * modes, width)[:, :n_grp * modes]
    for k in range(n_grp):
        part = lax.dot_general(
            through, sources[k * row_modes:(k + 1) * row_modes], LAST,
            precision=lax.Precision.HIGHEST, preferred_element_type=F32)
        part = part + jnp.where(g == k, lines[:, :row_modes], 0.0)
        upper, lower = split(part)
        t2[:n_high * modes, k * row_modes:(k + 1) * row_modes] = upper
        t2[n_high * modes:, k * row_modes:(k + 1) * row_modes] = lower

    for f in range(4):
        if f in shared:
            guard(f, lambda: basis_arrival(f).wait_recv())
            value = b_in[f] if f in (0, 2) else jnp.where(present[f], b_in[f], 0.0)
            upper, lower = split(value)
            bcat[f, 2 * modes:3 * modes, :] = upper
            bcat[f, 3 * modes:, :] = lower

    await_faces(0)
    for f in range(4):
        residual[f] = assembled(0, f)

    sol_out[...] = jnp.zeros((order, columns), F32)
    centre = jnp.full((1, columns), 0.5 * (spec[0] + spec[1]), F32)
    half_width = jnp.full((1, columns), 0.5 * (spec[1] - spec[0]), F32)
    third_rows = order // 3

    def to_local(total):
        for i in range(3):
            rows = slice(i * third_rows, (i + 1) * third_rows)
            out = dot_first(perm[:, rows], x2[...])
            xl2[rows, :] = out.astype(BF16)
            xl2[order + i * third_rows:order + (i + 1) * third_rows, :] = out.astype(BF16)
            if total is not None:
                total[rows, :] += halves(out)

    def precondition(r, c):
        for f in range(4):
            put(x2, slot_rows(f), residual[f] * weight[f])
        products = halves(dot(b2[...], x2[...]))
        plane[c, mine] = products[:modes, :] + products[modes:, :]
        for k in range(1, n_plane):
            plane_copy(c, k, mine).start()
        to_local(None)
        for i in range(3):
            rows = slice(i * third_rows, (i + 1) * third_rows)
            put(z2, rows, halves(dot(a2[rows, :], xl2[...])))
        for k in range(1, n_plane):
            plane_copy(c, k, from_plane(k)).wait_recv()
        put(c2, slice(None), plane[c].reshape(n_plane * modes, columns))
        parts = halves(dot(t2[...], c2[...]))
        parts = parts[:n_high * modes] + parts[n_high * modes:]
        part_out[c] = parts.reshape(n_high, modes, columns)
        for k in range(1, n_high):
            part_copy(c, k).start()
        for f in (0, 2, 3, 1):
            sendb[r, f] = halves(dot(perm[slot_rows(f), :], z2[...])) * weight[f]
            send_face(r, f)
        if c == 0:
            permute_schur(0, blocks // 2)
        update = part_out[c, high]
        for k in range(1, n_high):
            part_copy(c, k).wait_recv()
            update = update + part_in[c, k]
        x_out[c] = update
        for f in shared:
            guard(f, lambda: coarse_copy(c, f).start())
        if c == 0:
            permute_schur(blocks // 2, blocks)
        upper, lower = split(update)
        for f in range(4):
            for base in (0, modes):
                xcat[f, base:base + modes, :columns] = upper
                xcat[f, base:base + modes, columns:] = lower
        await_faces(r)
        for f in reversed(shared):
            guard(f, lambda: coarse_arrival(c, f).wait_recv())
        fields = []
        for f in range(4):
            rows = 2 * modes
            if f in shared:
                rows = 4 * modes
                value = x_in[c, f] if f in (0, 2) else jnp.where(present[f], x_in[c, f], 0.0)
                upper, lower = split(value)
                for base in (2 * modes, 3 * modes):
                    xcat[f, base:base + modes, :columns] = upper
                    xcat[f, base:base + modes, columns:] = lower
            coarse = halves(dot_first(bcat[f, :rows, :], xcat[f, :rows, :]))[:face]
            fields.append(assembled(r, f) + coarse * weight[f])
        return fields

    fields = precondition(1, 0)
    for f in range(4):
        direction[f] = fields[f] / centre
    rho = half_width / centre
    for turn in range(ITERS):
        for f in range(4):
            put(x2, slot_rows(f), direction[f])
        to_local(sol_out)
        r = 2 + 2 * turn
        for f in (0, 2, 3, 1):
            sendb[r, f] = halves(dot(sp2[slot_rows(f), :], xl2[...]))
            send_face(r, f)
        await_faces(r)
        for f in range(4):
            residual[f] = residual[f] - assembled(r, f)
        if turn + 1 < ITERS:
            rho_next = 1.0 / (2.0 * centre / half_width - rho)
            fields = precondition(r + 1, 1 + turn)
            for f in range(4):
                direction[f] = rho_next * rho * direction[f] + (2.0 * rho_next / half_width) * fields[f]
            rho = rho_next

    for f in range(4):
        put(x2, slot_rows(f), residual[f])
    for i in range(3):
        rows = slice(i * third_rows, (i + 1) * third_rows)
        res_out[rows, :] = halves(dot_first(perm[:, rows], x2[...]))

    for r in range(1 + 2 * ITERS):
        for f in shared:
            guard(f, lambda: face_copy(r, f).wait_send())
    for f in shared:
        guard(f, lambda: basis_copy(f).wait_send())
    for k in range(1, n_high):
        line_copy(k, high).wait_send()
    for k in range(1, n_plane):
        modes_copy(k, mine).wait_send()
    for c in range(ITERS):
        for k in range(1, n_plane):
            plane_copy(c, k, mine).wait_send()
        for k in range(1, n_high):
            part_copy(c, k).wait_send()
        for f in shared:
            guard(f, lambda: coarse_copy(c, f).wait_send())


def hand_out(sol, res, sol_out, res_out):
    sol_out[...] = sol[...]
    res_out[...] = res[...]


def solution(mesh):
    n_grp, n_sub = mesh.shape["grp"], mesh.shape["sub"]
    n_low = 1
    while n_low * n_low < n_sub:
        n_low *= 2
    n_high = n_sub // n_low
    n_plane = n_grp * n_low

    def step(load, schur, linv, basis, ginv, gm, top, fmap, spec):
        order, columns = load.shape
        modes = basis.shape[0]
        face = order // 4
        padded = -(-face // 128) * 128
        width = -(-n_grp * modes // 128) * 128
        faces = 1 + 2 * ITERS
        vmem = pl.BlockSpec(memory_space=pltpu.VMEM)
        hbm = pl.BlockSpec(memory_space=pl.ANY)
        smem = pl.BlockSpec(memory_space=pltpu.SMEM)
        dma = pltpu.SemaphoreType.DMA
        field = jax.ShapeDtypeStruct((order, columns), F32)
        sol, res = pl.pallas_call(
            functools.partial(kernel, n_grp, n_sub, n_low),
            out_shape=(field, field),
            in_specs=[hbm, hbm, hbm, vmem, vmem, vmem, vmem, vmem, smem],
            out_specs=(vmem, vmem),
            scratch_shapes=[
                pltpu.VMEM((order, columns), F32),
                pltpu.VMEM((order, order), F32),
                pltpu.VMEM((order, order), F32),
                pltpu.VMEM((order, 2 * order), BF16),
                pltpu.VMEM((order, 2 * order), BF16),
                pltpu.VMEM((order, 2 * order), BF16),
                pltpu.VMEM((order, order), BF16),
                pltpu.VMEM((order, 128), F32),
                pltpu.VMEM((2 * modes, order), BF16),
                pltpu.VMEM((4, 4 * modes, padded), BF16),
                pltpu.VMEM((order, 2 * columns), BF16),
                pltpu.VMEM((2 * order, 2 * columns), BF16),
                pltpu.VMEM((order, 2 * columns), BF16),
                pltpu.VMEM((4, 4 * modes, 2 * columns), BF16),
                pltpu.VMEM((4, face, columns), F32),
                pltpu.VMEM((4, face, columns), F32),
                pltpu.VMEM((faces, 4, face, columns), F32),
                pltpu.VMEM((faces, 4, face, columns), F32),
                pltpu.VMEM((4, modes, padded), F32),
                pltpu.VMEM((4, modes, padded), F32),
                pltpu.VMEM((n_high, modes, n_low * modes + 128), F32),
                pltpu.VMEM((n_high, modes, n_low * modes + 128), F32),
                pltpu.VMEM((n_plane, modes, width), F32),
                pltpu.VMEM((2 * n_high * modes, n_plane * modes), BF16),
                pltpu.VMEM((ITERS, n_plane, modes, columns), F32),
                pltpu.VMEM((n_plane * modes, 2 * columns), BF16),
                pltpu.VMEM((ITERS, n_high, modes, columns), F32),
                pltpu.VMEM((ITERS, n_high, modes, columns), F32),
                pltpu.VMEM((ITERS, modes, columns), F32),
                pltpu.VMEM((ITERS, 4, modes, columns), F32),
                dma((3,)),
                dma((faces, 4)),
                dma((faces, 4)),
                dma((1 + ITERS, n_plane)),
                dma((1 + ITERS, n_plane)),
                dma((1 + ITERS, n_high)),
                dma((1 + ITERS, n_high)),
                dma((1 + ITERS, 4)),
                dma((1 + ITERS, 4)),
            ],
            compiler_params=pltpu.CompilerParams(
                collective_id=0, has_side_effects=True, vmem_limit_bytes=60 * 1024 * 1024
            ),
        )(load, schur, linv, basis, ginv, gm, top, fmap, spec)
        return pl.pallas_call(
            hand_out, out_shape=(field, field), in_specs=[vmem, vmem], out_specs=(vmem, vmem)
        )(sol, res)

    row = P(("grp", "sub"), None)
    return jax.shard_map(
        step,
        mesh=mesh,
        in_specs=(row, row, row, row, row, row, P(), row, P()),
        out_specs=(row, row),
        check_vma=False,
    )
```

```python
import functools

import jax
import jax.numpy as jnp
from jax import lax
from jax.experimental import pallas as pl
from jax.experimental.pallas import tpu as pltpu
from jax.sharding import PartitionSpec as P

ITERS = 3
F32 = jnp.float32
BF16 = jnp.bfloat16
MESH = pl.DeviceIdType.MESH
FIRST = (((0,), (0,)), ((), ()))
LAST = (((1,), (1,)), ((), ()))


def dot(a, b):
    return jnp.dot(a, b, preferred_element_type=F32)


def dot_first(a, b):
    return lax.dot_general(a, b, FIRST, preferred_element_type=F32)


def dot_last(a, b):
    return lax.dot_general(a, b, LAST, preferred_element_type=F32)


def exact_dot(a, b):
    return jnp.dot(a, b, precision=lax.Precision.HIGHEST, preferred_element_type=F32)


def split(v):
    high = v.astype(BF16)
    low = (v - high.astype(F32)).astype(BF16)
    return high, low


def kernel(
    n_grp, n_sub, n_low,
    load, schur, linv, basis, ginv, gm, top, fmap, spec,
    sol_out, res_out,
    stage_l, stage_a, stage_s, a2, s2, sp2, perm, map_column, b2, gcat, x2, early, products, xl2, z2, xcat, direction, residual,
    sendb, recvb, b_out, b_in, line_out, line_in, plane_modes, t2, plane, c2, part_out, part_in, x_out, x_in,
    load_sem, face_send, face_recv, p_send, p_recv, z_send, z_recv, n_send, n_recv,
):
    order, columns = sol_out.shape
    face = order // 4
    modes = basis.shape[0]
    n_high = n_sub // n_low
    n_plane = n_grp * n_low
    row_modes = n_low * modes
    tile = 128
    g = lax.axis_index("grp")
    j = lax.axis_index("sub")
    high, low = j // n_low, j % n_low
    mine = g * n_low + low

    core = j % 2
    first = jnp.where(g == 0, 1, 0)
    face_of = [first, 2 + core, 1 - first, 3 - core]
    far = jnp.logical_or(jnp.logical_and(core == 0, j > 0), jnp.logical_and(core == 1, j < n_sub - 1))
    present = [True, far, jnp.logical_and(g > 0, g < n_grp - 1), True]
    peer = [{"grp": jnp.where(g == 0, 1, g - 1)}, {"sub": j - 1 + 2 * core}, {"grp": g + 1}, {"sub": j + 1 - 2 * core}]
    landing = [jnp.where(g >= 2, 2, 0) if n_grp > 2 else 0, 1, 0, 3]
    shared = [0] + ([1] if n_sub > 2 else []) + ([2] if n_grp > 2 else []) + [3]
    weight = [0.5, jnp.where(present[1], 0.5, 1.0).astype(F32) if n_sub > 2 else 1.0,
              jnp.where(present[2], 0.5, 1.0).astype(F32) if n_grp > 2 else 1.0, 0.5]
    always, late, soon = (0, 3), (0, 1), (2, 3)
    half = 2 * face

    def guard(f, action):
        if f in always:
            action()
        else:
            pl.when(present[f])(action)

    load_l = pltpu.make_async_copy(load, stage_l, load_sem.at[0])
    load_a = pltpu.make_async_copy(linv, stage_a, load_sem.at[1])
    load_s = pltpu.make_async_copy(schur, stage_s, load_sem.at[2])
    load_l.start()
    load_a.start()
    load_s.start()

    def plane_peer(k):
        q = lax.rem(mine + k, n_plane)
        return {"grp": q // n_low, "sub": high * n_low + lax.rem(q, n_low)}

    def line_at(k):
        return lax.rem(high + k, n_high)

    def line_peer(k):
        return {"sub": line_at(k) * n_low + low}

    barrier = pltpu.get_barrier_semaphore()
    for k in range(1, n_plane):
        pl.semaphore_signal(barrier, inc=1, device_id=plane_peer(k), device_id_type=MESH)
    for k in range(1, n_high):
        pl.semaphore_signal(barrier, inc=1, device_id=line_peer(k), device_id_type=MESH)
    for f in (1, 3):
        if f in shared:
            guard(f, lambda: pl.semaphore_signal(barrier, inc=1, device_id=peer[f], device_id_type=MESH))
    expected = n_plane - 1 + n_high - 1 + 1
    if 1 in shared:
        expected = expected + jnp.where(present[1], 1, 0)

    def remote(src, dst, send, recv, device):
        return pltpu.make_async_remote_copy(
            src_ref=src, dst_ref=dst, send_sem=send, recv_sem=recv, device_id=device, device_id_type=MESH)

    def face_copy(r, f):
        return remote(sendb.at[r, f], recvb.at[r, landing[f]], face_send.at[r, f], face_recv.at[r, landing[f]], peer[f])

    def face_arrival(r, f):
        return remote(sendb.at[r, f], recvb.at[r, f], face_send.at[r, f], face_recv.at[r, f], peer[f])

    def basis_copy(f):
        return remote(b_out.at[f], b_in.at[landing[f]], n_send.at[0, f], n_recv.at[0, landing[f]], peer[f])

    def basis_arrival(f):
        return remote(b_out.at[f], b_in.at[f], n_send.at[0, f], n_recv.at[0, f], peer[f])

    def coarse_copy(c, f):
        return remote(x_out.at[c], x_in.at[c, landing[f]], n_send.at[1 + c, f], n_recv.at[1 + c, landing[f]], peer[f])

    def coarse_arrival(c, f):
        return remote(x_out.at[c], x_in.at[c, f], n_send.at[1 + c, f], n_recv.at[1 + c, f], peer[f])

    def modes_copy(k, slot):
        return remote(plane_modes.at[slot], plane_modes.at[slot], p_send.at[0, k], p_recv.at[0, k], plane_peer(k))

    def plane_copy(c, k, slot):
        return remote(plane.at[c, slot], plane.at[c, slot], p_send.at[1 + c, k], p_recv.at[1 + c, k], plane_peer(k))

    def from_plane(k):
        return lax.rem(mine + n_plane - k, n_plane)

    def line_copy(k, slot):
        return remote(line_out.at[line_at(k)], line_in.at[slot], z_send.at[0, k], z_recv.at[0, k], line_peer(k))

    def part_copy(c, k):
        return remote(part_out.at[c, line_at(k)], part_in.at[c, k], z_send.at[1 + c, k], z_recv.at[1 + c, k], line_peer(k))

    def from_line(k):
        return lax.rem(high + n_high - k, n_high)

    def send_face(r, f):
        if f in shared:
            guard(f, lambda: face_copy(r, f).start())

    def await_faces(r, slots):
        for f in [f for f in reversed(slots) if f in shared]:
            guard(f, lambda: face_arrival(r, f).wait_recv())

    def received(r, f):
        if f not in shared:
            return None
        value = recvb[r, f]
        return value if f in always else jnp.where(present[f], value, 0.0)

    def assembled(r, f):
        value = received(r, f)
        return sendb[r, f] if value is None else sendb[r, f] + value

    def halves(out):
        return out[:, :columns] + out[:, columns:]

    def put(ref, rows, value):
        upper, lower = split(value)
        ref[rows, :columns] = upper
        ref[rows, columns:] = lower

    def slot_rows(f):
        return slice(f * face, (f + 1) * face)

    map_row = fmap[...].astype(F32)
    map_column[...] = jnp.broadcast_to(map_row, (tile, order)).T
    lanes = lax.broadcasted_iota(jnp.int32, (face, tile), 1).astype(F32)
    for f in range(4):
        own = map_column[pl.ds(pl.multiple_of(face_of[f] * face, 16), face), :]
        for t in range(order // tile):
            perm[slot_rows(f), t * tile:(t + 1) * tile] = jnp.where(own == lanes + float(t * tile), 1.0, 0.0).astype(BF16)

    width = plane_modes.shape[2]
    row = lax.broadcasted_iota(jnp.int32, (modes, width), 0)
    lane = lax.broadcasted_iota(jnp.int32, (modes, width), 1)
    plane_modes[mine] = exact_dot(gm[...], jnp.where(lane == row + g * modes, 1.0, 0.0).astype(F32))
    own_modes = jnp.concatenate([gm[...], jnp.zeros((modes, tile - modes), F32)], axis=1)
    for h in range(n_high):
        line_out[h, :, :row_modes] = ginv[:, h * row_modes:(h + 1) * row_modes]
        line_out[h, :, row_modes:] = own_modes

    pl.semaphore_wait(barrier, expected)

    for k in range(1, n_high):
        line_copy(k, high).start()
    for k in range(1, n_plane):
        modes_copy(k, mine).start()

    load_l.wait()
    for i in range(4):
        put(z2, slot_rows(i), stage_l[slot_rows(i), :])
    for f in (0, 1, 3, 2):
        sendb[0, f] = halves(dot(perm[slot_rows(f), :], z2[...]))
        send_face(0, f)

    upper, lower = split(basis[...])
    both = jnp.concatenate([upper, lower], axis=0)
    for part in range(2):
        b2[part] = dot_last(both, perm[part * half:(part + 1) * half, :]).astype(BF16)
    for f in range(4):
        moved = dot_last(both, perm[slot_rows(f), :])
        b_out[f] = jnp.zeros(b_out.shape[1:], F32)
        b_out[f, :, :face] = moved[:modes] + moved[modes:]
        if f in shared:
            guard(f, lambda: basis_copy(f).start())

    def split_matrix(stage, matrix):
        def chunk(i, carry):
            rows = pl.ds(pl.multiple_of(i * tile, tile), tile)
            upper, lower = split(stage[rows, :])
            matrix[rows, :order] = upper
            matrix[rows, order:] = lower
            return carry
        lax.fori_loop(0, order // tile, chunk, 0)

    def permute_schur(start, stop):
        for i in range(start, stop):
            lanes = slice(2 * i * tile, 2 * (i + 1) * tile)
            sp2[:, lanes] = dot(perm[...], s2[:, lanes]).astype(BF16)
    blocks = order // tile
    held = 1 + len(shared)

    def own_bases():
        position = lax.broadcasted_iota(jnp.int32, (16, order), 1)
        weights = jnp.full((16, order), weight[0], F32)
        for f in range(1, 4):
            weights = jnp.where(position >= f * face, weight[f], weights)
        weights = dot(weights.astype(BF16), perm[...])[:1]
        for part in range(2):
            rows = slice(part * held * modes, (part * held + 1) * modes)
            gcat[rows, :] = (both[part * modes:(part + 1) * modes].astype(F32) * weights).astype(BF16)

    def neighbour_bases():
        for n, f in enumerate(shared):
            guard(f, lambda: basis_arrival(f).wait_recv())
            value = b_in[f] if f in always else jnp.where(present[f], b_in[f], 0.0)
            upper, lower = split(value * weight[f])
            moved = dot(jnp.concatenate([upper, lower], axis=0)[:, :face], perm[slot_rows(f), :])
            for part in range(2):
                base = (part * held + 1 + n) * modes
                gcat[base:base + modes, :] = moved[part * modes:(part + 1) * modes].astype(BF16)

    load_a.wait()
    split_matrix(stage_a, a2)
    load_s.wait()
    split_matrix(stage_s, s2)

    line_in[high] = line_out[high]
    for k in range(1, n_high):
        line_copy(k, from_line(k)).wait_recv()
    for k in range(1, n_plane):
        modes_copy(k, from_plane(k)).wait_recv()
    lines = line_in[...].reshape(n_high * modes, row_modes + tile)
    top_rows = top[pl.ds(pl.multiple_of(g * modes, modes), modes), :]
    through = exact_dot(lines[:, row_modes:row_modes + modes], top_rows)
    sources = plane_modes[...].reshape(n_plane * modes, width)[:, :n_grp * modes]
    for k in range(n_grp):
        part = lax.dot_general(
            through, sources[k * row_modes:(k + 1) * row_modes], LAST,
            precision=lax.Precision.HIGHEST, preferred_element_type=F32)
        part = part + jnp.where(g == k, lines[:, :row_modes], 0.0)
        upper, lower = split(part)
        t2[:n_high * modes, k * row_modes:(k + 1) * row_modes] = upper
        t2[n_high * modes:, k * row_modes:(k + 1) * row_modes] = lower

    third_rows = order // 3

    def thirds():
        for i in range(3):
            yield (slice(i * third_rows, (i + 1) * third_rows),
                   slice(order + i * third_rows, order + (i + 1) * third_rows))

    def begin():
        for rows, _ in thirds():
            early[rows, :] = dot_first(perm[half:, rows], x2[half:, :])

    def complete(rows):
        return early[rows, :] + dot_first(perm[:half, rows], x2[:half, :])

    def update_residual(r, weighted):
        for slots in (soon, late):
            await_faces(r, slots)
            for f in slots:
                value = assembled(r, f) if r == 0 else residual[f] - assembled(r, f)
                residual[f] = value
                put(x2, slot_rows(f), value * weight[f] if weighted else value)
            if slots is soon:
                begin()
                if weighted:
                    products[...] = dot(b2[1], x2[half:, :])

    update_residual(0, True)
    centre = jnp.full((1, columns), 0.5 * (spec[0] + spec[1]), F32)
    half_width = jnp.full((1, columns), 0.5 * (spec[1] - spec[0]), F32)

    def precondition(r, c, step, keep):
        block = halves(products[...] + dot(b2[0], x2[:half, :]))
        plane[c, mine] = block[:modes, :] + block[modes:, :]
        for k in range(1, n_plane):
            plane_copy(c, k, mine).start()
        for rows, second in thirds():
            out = complete(rows).astype(BF16)
            xl2[rows, :] = out
            xl2[second, :] = out
        for rows, _ in thirds():
            put(z2, rows, halves(dot(a2[rows, :], xl2[...])))

        def outward(slots):
            for f in slots:
                sendb[r, f] = halves(dot(perm[slot_rows(f), :], z2[...])) * weight[f]
                send_face(r, f)
        outward((0, 1))
        for k in range(1, n_plane):
            plane_copy(c, k, from_plane(k)).wait_recv()
        put(c2, slice(None), plane[c].reshape(n_plane * modes, columns))
        parts = halves(dot(t2[...], c2[...]))
        parts = parts[:n_high * modes] + parts[n_high * modes:]
        part_out[c] = parts.reshape(n_high, modes, columns)
        for k in range(1, n_high):
            part_copy(c, k).start()
        outward((3, 2))
        if c == 0:
            own_bases()
            neighbour_bases()
            permute_schur(0, blocks // 3)
        await_faces(r, soon)
        for f in soon:
            put(x2, slot_rows(f), assembled(r, f))
        begin()
        update = part_out[c, high]
        for k in range(1, n_high):
            part_copy(c, k).wait_recv()
            update = update + part_in[c, k]
        x_out[c] = update
        for f in shared:
            guard(f, lambda: coarse_copy(c, f).start())
        if c == 0:
            permute_schur(blocks // 3, blocks)

        def place(n, value):
            upper, lower = split(value)
            for base in (n * modes, (held + n) * modes):
                xcat[base:base + modes, :columns] = upper
                xcat[base:base + modes, columns:] = lower
        place(0, update)
        await_faces(r, late)
        for f in late:
            put(x2, slot_rows(f), assembled(r, f))
        for rows, _ in thirds():
            value = halves(complete(rows)) * step
            if keep is not None:
                value = value + direction[rows, :] * keep
            direction[rows, :] = value
        for f in reversed(shared):
            guard(f, lambda: coarse_arrival(c, f).wait_recv())
        for n, f in enumerate(shared):
            place(1 + n, x_in[c, f] if f in always else jnp.where(present[f], x_in[c, f], 0.0))
        for rows, second in thirds():
            value = direction[rows, :] + halves(dot_first(gcat[:, rows], xcat[...])) * step
            direction[rows, :] = value
            upper, lower = split(value)
            for part in (rows, second):
                xl2[part, :columns] = upper
                xl2[part, columns:] = lower

    precondition(1, 0, 1.0 / centre, None)
    rho = half_width / centre
    for turn in range(ITERS):
        r = 2 + 2 * turn
        for f in (0, 1, 3, 2):
            sendb[r, f] = halves(dot(sp2[slot_rows(f), :], xl2[...]))
            send_face(r, f)
        sol_out[...] = direction[...] if turn == 0 else sol_out[...] + direction[...]
        update_residual(r, turn + 1 < ITERS)
        if turn + 1 < ITERS:
            rho_next = 1.0 / (2.0 * centre / half_width - rho)
            precondition(r + 1, 1 + turn, 2.0 * rho_next / half_width, rho_next * rho)
            rho = rho_next

    for rows, _ in thirds():
        res_out[rows, :] = halves(complete(rows))

    for r in range(1 + 2 * ITERS):
        for f in shared:
            guard(f, lambda: face_copy(r, f).wait_send())
    for f in shared:
        guard(f, lambda: basis_copy(f).wait_send())
    for k in range(1, n_high):
        line_copy(k, high).wait_send()
    for k in range(1, n_plane):
        modes_copy(k, mine).wait_send()
    for c in range(ITERS):
        for k in range(1, n_plane):
            plane_copy(c, k, mine).wait_send()
        for k in range(1, n_high):
            part_copy(c, k).wait_send()
        for f in shared:
            guard(f, lambda: coarse_copy(c, f).wait_send())


def hand_out(sol, res, sol_out, res_out):
    sol_out[...] = sol[...]
    res_out[...] = res[...]


def solution(mesh):
    n_grp, n_sub = mesh.shape["grp"], mesh.shape["sub"]
    n_low = 1
    while n_low * n_low < n_sub:
        n_low *= 2
    n_high = n_sub // n_low
    n_plane = n_grp * n_low
    held = 3 + (1 if n_grp > 2 else 0) + (1 if n_sub > 2 else 0)

    def step(load, schur, linv, basis, ginv, gm, top, fmap, spec):
        order, columns = load.shape
        modes = basis.shape[0]
        face = order // 4
        padded = -(-face // 128) * 128
        width = -(-n_grp * modes // 128) * 128
        faces = 1 + 2 * ITERS
        vmem = pl.BlockSpec(memory_space=pltpu.VMEM)
        hbm = pl.BlockSpec(memory_space=pl.ANY)
        smem = pl.BlockSpec(memory_space=pltpu.SMEM)
        dma = pltpu.SemaphoreType.DMA
        field = jax.ShapeDtypeStruct((order, columns), F32)
        sol, res = pl.pallas_call(
            functools.partial(kernel, n_grp, n_sub, n_low),
            out_shape=(field, field),
            in_specs=[hbm, hbm, hbm, vmem, vmem, vmem, vmem, vmem, smem],
            out_specs=(vmem, vmem),
            scratch_shapes=[
                pltpu.VMEM((order, columns), F32),
                pltpu.VMEM((order, order), F32),
                pltpu.VMEM((order, order), F32),
                pltpu.VMEM((order, 2 * order), BF16),
                pltpu.VMEM((order, 2 * order), BF16),
                pltpu.VMEM((order, 2 * order), BF16),
                pltpu.VMEM((order, order), BF16),
                pltpu.VMEM((order, 128), F32),
                pltpu.VMEM((2, 2 * modes, 2 * face), BF16),
                pltpu.VMEM((2 * held * modes, order), BF16),
                pltpu.VMEM((order, 2 * columns), BF16),
                pltpu.VMEM((order, 2 * columns), F32),
                pltpu.VMEM((2 * modes, 2 * columns), F32),
                pltpu.VMEM((2 * order, 2 * columns), BF16),
                pltpu.VMEM((order, 2 * columns), BF16),
                pltpu.VMEM((2 * held * modes, 2 * columns), BF16),
                pltpu.VMEM((order, columns), F32),
                pltpu.VMEM((4, face, columns), F32),
                pltpu.VMEM((faces, 4, face, columns), F32),
                pltpu.VMEM((faces, 4, face, columns), F32),
                pltpu.VMEM((4, modes, padded), F32),
                pltpu.VMEM((4, modes, padded), F32),
                pltpu.VMEM((n_high, modes, n_low * modes + 128), F32),
                pltpu.VMEM((n_high, modes, n_low * modes + 128), F32),
                pltpu.VMEM((n_plane, modes, width), F32),
                pltpu.VMEM((2 * n_high * modes, n_plane * modes), BF16),
                pltpu.VMEM((ITERS, n_plane, modes, columns), F32),
                pltpu.VMEM((n_plane * modes, 2 * columns), BF16),
                pltpu.VMEM((ITERS, n_high, modes, columns), F32),
                pltpu.VMEM((ITERS, n_high, modes, columns), F32),
                pltpu.VMEM((ITERS, modes, columns), F32),
                pltpu.VMEM((ITERS, 4, modes, columns), F32),
                dma((3,)),
                dma((faces, 4)),
                dma((faces, 4)),
                dma((1 + ITERS, n_plane)),
                dma((1 + ITERS, n_plane)),
                dma((1 + ITERS, n_high)),
                dma((1 + ITERS, n_high)),
                dma((1 + ITERS, 4)),
                dma((1 + ITERS, 4)),
            ],
            compiler_params=pltpu.CompilerParams(
                collective_id=0, has_side_effects=True, vmem_limit_bytes=60 * 1024 * 1024
            ),
        )(load, schur, linv, basis, ginv, gm, top, fmap, spec)
        return pl.pallas_call(
            hand_out, out_shape=(field, field), in_specs=[vmem, vmem], out_specs=(vmem, vmem)
        )(sol, res)

    row = P(("grp", "sub"), None)
    return jax.shard_map(
        step,
        mesh=mesh,
        in_specs=(row, row, row, row, row, row, P(), row, P()),
        out_specs=(row, row),
        check_vma=False,
    )
```

```python
import functools

import jax
import jax.numpy as jnp
from jax import lax
from jax.experimental import pallas as pl
from jax.experimental.pallas import tpu as pltpu
from jax.sharding import PartitionSpec as P

ITERS = 3
F32 = jnp.float32
BF16 = jnp.bfloat16
MESH = pl.DeviceIdType.MESH
FIRST = (((0,), (0,)), ((), ()))
LAST = (((1,), (1,)), ((), ()))


def dot(a, b):
    return jnp.dot(a, b, preferred_element_type=F32)


def dot_first(a, b):
    return lax.dot_general(a, b, FIRST, preferred_element_type=F32)


def dot_last(a, b):
    return lax.dot_general(a, b, LAST, preferred_element_type=F32)


def exact_dot(a, b):
    return jnp.dot(a, b, precision=lax.Precision.HIGHEST, preferred_element_type=F32)


def split(v):
    high = v.astype(BF16)
    low = (v - high.astype(F32)).astype(BF16)
    return high, low


def kernel(
    n_grp, n_sub, n_low,
    load, schur, linv, basis, ginv, gm, top, fmap, spec,
    sol_out, res_out,
    stage_l, stage_a, stage_s, a2, s2, sp2, perm, map_column, b2, gcat, x2, early, products, xl2, z2, xcat, direction, residual,
    sendb, recvb, b_out, b_in, line_out, line_in, plane_modes, t2, plane, c2, part_out, part_in, x_out, x_in,
    load_sem, face_send, face_recv, p_send, p_recv, z_send, z_recv, n_send, n_recv,
):
    order, columns = sol_out.shape
    face = order // 4
    modes = basis.shape[0]
    n_high = n_sub // n_low
    n_plane = n_grp * n_low
    row_modes = n_low * modes
    tile = 128
    g = lax.axis_index("grp")
    j = lax.axis_index("sub")
    high, low = j // n_low, j % n_low
    mine = g * n_low + low

    core = j % 2
    first = jnp.where(g == 0, 1, 0)
    face_of = [first, 2 + core, 1 - first, 3 - core]
    far = jnp.logical_or(jnp.logical_and(core == 0, j > 0), jnp.logical_and(core == 1, j < n_sub - 1))
    present = [True, far, jnp.logical_and(g > 0, g < n_grp - 1), True]
    peer = [{"grp": jnp.where(g == 0, 1, g - 1)}, {"sub": j - 1 + 2 * core}, {"grp": g + 1}, {"sub": j + 1 - 2 * core}]
    landing = [jnp.where(g >= 2, 2, 0) if n_grp > 2 else 0, 1, 0, 3]
    shared = [0] + ([1] if n_sub > 2 else []) + ([2] if n_grp > 2 else []) + [3]
    weight = [0.5, jnp.where(present[1], 0.5, 1.0).astype(F32) if n_sub > 2 else 1.0,
              jnp.where(present[2], 0.5, 1.0).astype(F32) if n_grp > 2 else 1.0, 0.5]
    always, late, soon = (0, 3), (0, 1), (2, 3)
    half = 2 * face

    def guard(f, action):
        if f in always:
            action()
        else:
            pl.when(present[f])(action)

    load_l = pltpu.make_async_copy(load, stage_l, load_sem.at[0])
    load_a = pltpu.make_async_copy(linv, stage_a, load_sem.at[1])
    load_s = pltpu.make_async_copy(schur, stage_s, load_sem.at[2])
    load_l.start()
    load_a.start()
    load_s.start()

    def plane_peer(k):
        q = lax.rem(mine + k, n_plane)
        return {"grp": q // n_low, "sub": high * n_low + lax.rem(q, n_low)}

    def line_at(k):
        return lax.rem(high + k, n_high)

    def line_peer(k):
        return {"sub": line_at(k) * n_low + low}

    barrier = pltpu.get_barrier_semaphore()
    for k in range(1, n_plane):
        pl.semaphore_signal(barrier, inc=1, device_id=plane_peer(k), device_id_type=MESH)
    for k in range(1, n_high):
        pl.semaphore_signal(barrier, inc=1, device_id=line_peer(k), device_id_type=MESH)
    for f in (1, 3):
        if f in shared:
            guard(f, lambda: pl.semaphore_signal(barrier, inc=1, device_id=peer[f], device_id_type=MESH))
    expected = n_plane - 1 + n_high - 1 + 1
    if 1 in shared:
        expected = expected + jnp.where(present[1], 1, 0)

    def remote(src, dst, send, recv, device):
        return pltpu.make_async_remote_copy(
            src_ref=src, dst_ref=dst, send_sem=send, recv_sem=recv, device_id=device, device_id_type=MESH)

    def face_copy(r, f):
        return remote(sendb.at[r, f], recvb.at[r, landing[f]], face_send.at[r, f], face_recv.at[r, landing[f]], peer[f])

    def face_arrival(r, f):
        return remote(sendb.at[r, f], recvb.at[r, f], face_send.at[r, f], face_recv.at[r, f], peer[f])

    def basis_copy(f):
        return remote(b_out.at[f], b_in.at[landing[f]], n_send.at[0, f], n_recv.at[0, landing[f]], peer[f])

    def basis_arrival(f):
        return remote(b_out.at[f], b_in.at[f], n_send.at[0, f], n_recv.at[0, f], peer[f])

    def coarse_copy(c, f):
        return remote(x_out.at[c], x_in.at[c, landing[f]], n_send.at[1 + c, f], n_recv.at[1 + c, landing[f]], peer[f])

    def coarse_arrival(c, f):
        return remote(x_out.at[c], x_in.at[c, f], n_send.at[1 + c, f], n_recv.at[1 + c, f], peer[f])

    def modes_copy(k, slot):
        return remote(plane_modes.at[slot], plane_modes.at[slot], p_send.at[0, k], p_recv.at[0, k], plane_peer(k))

    def plane_copy(c, k, slot):
        return remote(plane.at[c, slot], plane.at[c, slot], p_send.at[1 + c, k], p_recv.at[1 + c, k], plane_peer(k))

    def from_plane(k):
        return lax.rem(mine + n_plane - k, n_plane)

    def line_copy(k, slot):
        return remote(line_out.at[line_at(k)], line_in.at[slot], z_send.at[0, k], z_recv.at[0, k], line_peer(k))

    def part_copy(c, k):
        return remote(part_out.at[c, line_at(k)], part_in.at[c, k], z_send.at[1 + c, k], z_recv.at[1 + c, k], line_peer(k))

    def from_line(k):
        return lax.rem(high + n_high - k, n_high)

    def send_face(r, f):
        if f in shared:
            guard(f, lambda: face_copy(r, f).start())

    def await_faces(r, slots):
        for f in [f for f in reversed(slots) if f in shared]:
            guard(f, lambda: face_arrival(r, f).wait_recv())

    def received(r, f):
        if f not in shared:
            return None
        value = recvb[r, f]
        return value if f in always else jnp.where(present[f], value, 0.0)

    def assembled(r, f):
        value = received(r, f)
        return sendb[r, f] if value is None else sendb[r, f] + value

    def halves(out):
        return out[:, :columns] + out[:, columns:]

    def put(ref, rows, value):
        upper, lower = split(value)
        ref[rows, :columns] = upper
        ref[rows, columns:] = lower

    def slot_rows(f):
        return slice(f * face, (f + 1) * face)

    map_row = fmap[...].astype(F32)
    map_column[...] = jnp.broadcast_to(map_row, (tile, order)).T
    lanes = lax.broadcasted_iota(jnp.int32, (face, tile), 1).astype(F32)
    for f in range(4):
        own = map_column[pl.ds(pl.multiple_of(face_of[f] * face, 16), face), :]
        for t in range(order // tile):
            perm[slot_rows(f), t * tile:(t + 1) * tile] = jnp.where(own == lanes + float(t * tile), 1.0, 0.0).astype(BF16)

    width = plane_modes.shape[2]
    row = lax.broadcasted_iota(jnp.int32, (modes, width), 0)
    lane = lax.broadcasted_iota(jnp.int32, (modes, width), 1)
    plane_modes[mine] = exact_dot(gm[...], jnp.where(lane == row + g * modes, 1.0, 0.0).astype(F32))
    own_modes = jnp.concatenate([gm[...], jnp.zeros((modes, tile - modes), F32)], axis=1)
    for h in range(n_high):
        line_out[h, :, :row_modes] = ginv[:, h * row_modes:(h + 1) * row_modes]
        line_out[h, :, row_modes:] = own_modes

    pl.semaphore_wait(barrier, expected)

    load_l.wait()
    for i in range(4):
        put(z2, slot_rows(i), stage_l[slot_rows(i), :])
    for f in (0, 1, 3, 2):
        sendb[0, f] = halves(dot(perm[slot_rows(f), :], z2[...]))
        send_face(0, f)

    for k in range(1, n_high):
        line_copy(k, high).start()
    for k in range(1, n_plane):
        modes_copy(k, mine).start()

    upper, lower = split(basis[...])
    both = jnp.concatenate([upper, lower], axis=0)
    for part in range(2):
        b2[part] = dot_last(both, perm[part * half:(part + 1) * half, :]).astype(BF16)
    for f in range(4):
        moved = dot_last(both, perm[slot_rows(f), :])
        b_out[f] = jnp.zeros(b_out.shape[1:], F32)
        b_out[f, :, :face] = moved[:modes] + moved[modes:]
        if f in shared:
            guard(f, lambda: basis_copy(f).start())

    def split_matrix(stage, matrix):
        def chunk(i, carry):
            rows = pl.ds(pl.multiple_of(i * tile, tile), tile)
            upper, lower = split(stage[rows, :])
            matrix[rows, :order] = upper
            matrix[rows, order:] = lower
            return carry
        lax.fori_loop(0, order // tile, chunk, 0)

    def permute_schur(start, stop):
        for i in range(start, stop):
            rows = slice(i // blocks * half, (i // blocks + 1) * half)
            lanes = slice(2 * (i % blocks) * tile, 2 * (i % blocks + 1) * tile)
            sp2[rows, lanes] = dot(perm[rows, :], s2[:, lanes]).astype(BF16)
    blocks = order // tile
    stages = [blocks // 2, blocks * 3 // 4, blocks * 4 // 3, 2 * blocks]
    held = 1 + len(shared)

    def own_bases():
        position = lax.broadcasted_iota(jnp.int32, (16, order), 1)
        weights = jnp.full((16, order), weight[0], F32)
        for f in range(1, 4):
            weights = jnp.where(position >= f * face, weight[f], weights)
        weights = dot(weights.astype(BF16), perm[...])[:1]
        for part in range(2):
            rows = slice(part * held * modes, (part * held + 1) * modes)
            gcat[rows, :] = (both[part * modes:(part + 1) * modes].astype(F32) * weights).astype(BF16)

    def neighbour_bases():
        for n, f in enumerate(shared):
            guard(f, lambda: basis_arrival(f).wait_recv())
            value = b_in[f] if f in always else jnp.where(present[f], b_in[f], 0.0)
            upper, lower = split(value * weight[f])
            moved = dot(jnp.concatenate([upper, lower], axis=0)[:, :face], perm[slot_rows(f), :])
            for part in range(2):
                base = (part * held + 1 + n) * modes
                gcat[base:base + modes, :] = moved[part * modes:(part + 1) * modes].astype(BF16)

    load_a.wait()
    split_matrix(stage_a, a2)
    load_s.wait()
    split_matrix(stage_s, s2)

    permute_schur(0, stages[0])

    third_rows = order // 3

    def thirds():
        for i in range(3):
            yield (slice(i * third_rows, (i + 1) * third_rows),
                   slice(order + i * third_rows, order + (i + 1) * third_rows))

    def begin():
        for rows, _ in thirds():
            early[rows, :] = dot_first(perm[half:, rows], x2[half:, :])

    def complete(rows):
        return early[rows, :] + dot_first(perm[:half, rows], x2[:half, :])

    def update_residual(r, weighted):
        for slots in (soon, late):
            await_faces(r, slots)
            for f in slots:
                value = assembled(r, f) if r == 0 else residual[f] - assembled(r, f)
                residual[f] = value
                put(x2, slot_rows(f), value * weight[f] if weighted else value)
            if slots is soon:
                begin()
                if weighted:
                    products[...] = dot(b2[1], x2[half:, :])

    update_residual(0, True)
    centre = jnp.full((1, columns), 0.5 * (spec[0] + spec[1]), F32)
    half_width = jnp.full((1, columns), 0.5 * (spec[1] - spec[0]), F32)

    def build_coarse():
        line_in[high] = line_out[high]
        for k in range(1, n_high):
            line_copy(k, from_line(k)).wait_recv()
        for k in range(1, n_plane):
            modes_copy(k, from_plane(k)).wait_recv()
        lines = line_in[...].reshape(n_high * modes, row_modes + tile)
        top_rows = top[pl.ds(pl.multiple_of(g * modes, modes), modes), :]
        through = exact_dot(lines[:, row_modes:row_modes + modes], top_rows)
        sources = plane_modes[...].reshape(n_plane * modes, width)[:, :n_grp * modes]
        for k in range(n_grp):
            part = lax.dot_general(
                through, sources[k * row_modes:(k + 1) * row_modes], LAST,
                precision=lax.Precision.HIGHEST, preferred_element_type=F32)
            part = part + jnp.where(g == k, lines[:, :row_modes], 0.0)
            upper, lower = split(part)
            t2[:n_high * modes, k * row_modes:(k + 1) * row_modes] = upper
            t2[n_high * modes:, k * row_modes:(k + 1) * row_modes] = lower

    def precondition(r, c, step, keep):
        block = halves(products[...] + dot(b2[0], x2[:half, :]))
        plane[c, mine] = block[:modes, :] + block[modes:, :]
        for k in range(1, n_plane):
            plane_copy(c, k, mine).start()
        for rows, second in thirds():
            out = complete(rows).astype(BF16)
            xl2[rows, :] = out
            xl2[second, :] = out
        for rows, _ in thirds():
            put(z2, rows, halves(dot(a2[rows, :], xl2[...])))

        def outward(slots):
            for f in slots:
                sendb[r, f] = halves(dot(perm[slot_rows(f), :], z2[...])) * weight[f]
                send_face(r, f)
        if c == 0:
            build_coarse()
        for k in range(1, n_plane):
            plane_copy(c, k, from_plane(k)).wait_recv()
        put(c2, slice(None), plane[c].reshape(n_plane * modes, columns))
        parts = halves(dot(t2[...], c2[...]))
        parts = parts[:n_high * modes] + parts[n_high * modes:]
        part_out[c] = parts.reshape(n_high, modes, columns)
        for k in range(1, n_high):
            part_copy(c, k).start()
        outward((0, 1, 3, 2))
        if c == 0:
            own_bases()
            neighbour_bases()
            permute_schur(stages[0], stages[1])
        await_faces(r, soon)
        for f in soon:
            put(x2, slot_rows(f), assembled(r, f))
        begin()
        update = part_out[c, high]
        for k in range(1, n_high):
            part_copy(c, k).wait_recv()
            update = update + part_in[c, k]
        x_out[c] = update
        for f in shared:
            guard(f, lambda: coarse_copy(c, f).start())
        if c == 0:
            permute_schur(stages[1], stages[2])

        def place(n, value):
            upper, lower = split(value)
            for base in (n * modes, (held + n) * modes):
                xcat[base:base + modes, :columns] = upper
                xcat[base:base + modes, columns:] = lower
        place(0, update)
        await_faces(r, late)
        for f in late:
            put(x2, slot_rows(f), assembled(r, f))
        for rows, _ in thirds():
            value = halves(complete(rows)) * step
            if keep is not None:
                value = value + direction[rows, :] * keep
            direction[rows, :] = value
        for f in reversed(shared):
            guard(f, lambda: coarse_arrival(c, f).wait_recv())
        for n, f in enumerate(shared):
            place(1 + n, x_in[c, f] if f in always else jnp.where(present[f], x_in[c, f], 0.0))
        for rows, second in thirds():
            value = direction[rows, :] + halves(dot_first(gcat[:, rows], xcat[...])) * step
            direction[rows, :] = value
            upper, lower = split(value)
            for part in (rows, second):
                xl2[part, :columns] = upper
                xl2[part, columns:] = lower

    precondition(1, 0, 1.0 / centre, None)
    rho = half_width / centre
    for turn in range(ITERS):
        r = 2 + 2 * turn
        for f in (0, 1, 3, 2):
            if turn == 0 and f == 3:
                permute_schur(stages[2], stages[3])
            sendb[r, f] = halves(dot(sp2[slot_rows(f), :], xl2[...]))
            send_face(r, f)
        sol_out[...] = direction[...] if turn == 0 else sol_out[...] + direction[...]
        update_residual(r, turn + 1 < ITERS)
        if turn + 1 < ITERS:
            rho_next = 1.0 / (2.0 * centre / half_width - rho)
            precondition(r + 1, 1 + turn, 2.0 * rho_next / half_width, rho_next * rho)
            rho = rho_next

    for rows, _ in thirds():
        res_out[rows, :] = halves(complete(rows))

    for r in range(1 + 2 * ITERS):
        for f in shared:
            guard(f, lambda: face_copy(r, f).wait_send())
    for f in shared:
        guard(f, lambda: basis_copy(f).wait_send())
    for k in range(1, n_high):
        line_copy(k, high).wait_send()
    for k in range(1, n_plane):
        modes_copy(k, mine).wait_send()
    for c in range(ITERS):
        for k in range(1, n_plane):
            plane_copy(c, k, mine).wait_send()
        for k in range(1, n_high):
            part_copy(c, k).wait_send()
        for f in shared:
            guard(f, lambda: coarse_copy(c, f).wait_send())


def hand_out(sol, res, sol_out, res_out):
    sol_out[...] = sol[...]
    res_out[...] = res[...]


def solution(mesh):
    n_grp, n_sub = mesh.shape["grp"], mesh.shape["sub"]
    n_low = 1
    while n_low * n_low < n_sub:
        n_low *= 2
    n_high = n_sub // n_low
    n_plane = n_grp * n_low
    held = 3 + (1 if n_grp > 2 else 0) + (1 if n_sub > 2 else 0)

    def step(load, schur, linv, basis, ginv, gm, top, fmap, spec):
        order, columns = load.shape
        modes = basis.shape[0]
        face = order // 4
        padded = -(-face // 128) * 128
        width = -(-n_grp * modes // 128) * 128
        faces = 1 + 2 * ITERS
        vmem = pl.BlockSpec(memory_space=pltpu.VMEM)
        hbm = pl.BlockSpec(memory_space=pl.ANY)
        smem = pl.BlockSpec(memory_space=pltpu.SMEM)
        dma = pltpu.SemaphoreType.DMA
        field = jax.ShapeDtypeStruct((order, columns), F32)
        sol, res = pl.pallas_call(
            functools.partial(kernel, n_grp, n_sub, n_low),
            out_shape=(field, field),
            in_specs=[hbm, hbm, hbm, vmem, vmem, vmem, vmem, vmem, smem],
            out_specs=(vmem, vmem),
            scratch_shapes=[
                pltpu.VMEM((order, columns), F32),
                pltpu.VMEM((order, order), F32),
                pltpu.VMEM((order, order), F32),
                pltpu.VMEM((order, 2 * order), BF16),
                pltpu.VMEM((order, 2 * order), BF16),
                pltpu.VMEM((order, 2 * order), BF16),
                pltpu.VMEM((order, order), BF16),
                pltpu.VMEM((order, 128), F32),
                pltpu.VMEM((2, 2 * modes, 2 * face), BF16),
                pltpu.VMEM((2 * held * modes, order), BF16),
                pltpu.VMEM((order, 2 * columns), BF16),
                pltpu.VMEM((order, 2 * columns), F32),
                pltpu.VMEM((2 * modes, 2 * columns), F32),
                pltpu.VMEM((2 * order, 2 * columns), BF16),
                pltpu.VMEM((order, 2 * columns), BF16),
                pltpu.VMEM((2 * held * modes, 2 * columns), BF16),
                pltpu.VMEM((order, columns), F32),
                pltpu.VMEM((4, face, columns), F32),
                pltpu.VMEM((faces, 4, face, columns), F32),
                pltpu.VMEM((faces, 4, face, columns), F32),
                pltpu.VMEM((4, modes, padded), F32),
                pltpu.VMEM((4, modes, padded), F32),
                pltpu.VMEM((n_high, modes, n_low * modes + 128), F32),
                pltpu.VMEM((n_high, modes, n_low * modes + 128), F32),
                pltpu.VMEM((n_plane, modes, width), F32),
                pltpu.VMEM((2 * n_high * modes, n_plane * modes), BF16),
                pltpu.VMEM((ITERS, n_plane, modes, columns), F32),
                pltpu.VMEM((n_plane * modes, 2 * columns), BF16),
                pltpu.VMEM((ITERS, n_high, modes, columns), F32),
                pltpu.VMEM((ITERS, n_high, modes, columns), F32),
                pltpu.VMEM((ITERS, modes, columns), F32),
                pltpu.VMEM((ITERS, 4, modes, columns), F32),
                dma((3,)),
                dma((faces, 4)),
                dma((faces, 4)),
                dma((1 + ITERS, n_plane)),
                dma((1 + ITERS, n_plane)),
                dma((1 + ITERS, n_high)),
                dma((1 + ITERS, n_high)),
                dma((1 + ITERS, 4)),
                dma((1 + ITERS, 4)),
            ],
            compiler_params=pltpu.CompilerParams(
                collective_id=0, has_side_effects=True, vmem_limit_bytes=60 * 1024 * 1024
            ),
        )(load, schur, linv, basis, ginv, gm, top, fmap, spec)
        return pl.pallas_call(
            hand_out, out_shape=(field, field), in_specs=[vmem, vmem], out_specs=(vmem, vmem)
        )(sol, res)

    row = P(("grp", "sub"), None)
    return jax.shard_map(
        step,
        mesh=mesh,
        in_specs=(row, row, row, row, row, row, P(), row, P()),
        out_specs=(row, row),
        check_vma=False,
    )
```

```python
import functools

import jax
import jax.numpy as jnp
from jax import lax
from jax.experimental import pallas as pl
from jax.experimental.pallas import tpu as pltpu
from jax.sharding import PartitionSpec as P

ITERS = 3
F32 = jnp.float32
BF16 = jnp.bfloat16
MESH = pl.DeviceIdType.MESH
FIRST = (((0,), (0,)), ((), ()))
LAST = (((1,), (1,)), ((), ()))


def dot(a, b):
    return jnp.dot(a, b, preferred_element_type=F32)


def dot_first(a, b):
    return lax.dot_general(a, b, FIRST, preferred_element_type=F32)


def dot_last(a, b):
    return lax.dot_general(a, b, LAST, preferred_element_type=F32)


def exact_dot(a, b):
    return jnp.dot(a, b, precision=lax.Precision.HIGHEST, preferred_element_type=F32)


def split(v):
    high = v.astype(BF16)
    low = (v - high.astype(F32)).astype(BF16)
    return high, low


def kernel(
    n_grp, n_sub, n_low,
    load, schur, linv, basis, ginv, gm, top, fmap, spec,
    sol_out, res_out,
    total, stage_l, stage_a, stage_s, a2, s2, sp2, perm, map_column, b2, gcat, x2, early, products, xl2, z2, xcat, direction, residual,
    sendb, recvb, b_out, b_in, line_out, line_in, plane_modes, t2, plane, c2, part_out, part_in, x_out, x_in,
    load_sem, out_sem, face_send, face_recv, p_send, p_recv, z_send, z_recv, n_send, n_recv,
):
    order, columns = sol_out.shape
    face = order // 4
    modes = basis.shape[0]
    n_high = n_sub // n_low
    n_plane = n_grp * n_low
    row_modes = n_low * modes
    tile = 128
    g = lax.axis_index("grp")
    j = lax.axis_index("sub")
    high, low = j // n_low, j % n_low
    mine = g * n_low + low

    core = j % 2
    first = jnp.where(g == 0, 1, 0)
    face_of = [first, 2 + core, 1 - first, 3 - core]
    far = jnp.logical_or(jnp.logical_and(core == 0, j > 0), jnp.logical_and(core == 1, j < n_sub - 1))
    present = [True, far, jnp.logical_and(g > 0, g < n_grp - 1), True]
    peer = [{"grp": jnp.where(g == 0, 1, g - 1)}, {"sub": j - 1 + 2 * core}, {"grp": g + 1}, {"sub": j + 1 - 2 * core}]
    landing = [jnp.where(g >= 2, 2, 0) if n_grp > 2 else 0, 1, 0, 3]
    shared = [0] + ([1] if n_sub > 2 else []) + ([2] if n_grp > 2 else []) + [3]
    weight = [0.5, jnp.where(present[1], 0.5, 1.0).astype(F32) if n_sub > 2 else 1.0,
              jnp.where(present[2], 0.5, 1.0).astype(F32) if n_grp > 2 else 1.0, 0.5]
    always, late, soon = (0, 3), (0, 1), (2, 3)
    half = 2 * face

    def guard(f, action):
        if f in always:
            action()
        else:
            pl.when(present[f])(action)

    load_l = pltpu.make_async_copy(load, stage_l, load_sem.at[0])
    load_a = pltpu.make_async_copy(linv, stage_a, load_sem.at[1])
    load_s = pltpu.make_async_copy(schur, stage_s, load_sem.at[2])
    hand_total = pltpu.make_async_copy(total, sol_out, out_sem.at[0])
    load_l.start()
    load_a.start()
    load_s.start()

    def plane_peer(k):
        q = lax.rem(mine + k, n_plane)
        return {"grp": q // n_low, "sub": high * n_low + lax.rem(q, n_low)}

    def line_at(k):
        return lax.rem(high + k, n_high)

    def line_peer(k):
        return {"sub": line_at(k) * n_low + low}

    barrier = pltpu.get_barrier_semaphore()
    for k in range(1, n_plane):
        pl.semaphore_signal(barrier, inc=1, device_id=plane_peer(k), device_id_type=MESH)
    for k in range(1, n_high):
        pl.semaphore_signal(barrier, inc=1, device_id=line_peer(k), device_id_type=MESH)
    for f in (1, 3):
        if f in shared:
            guard(f, lambda: pl.semaphore_signal(barrier, inc=1, device_id=peer[f], device_id_type=MESH))
    expected = n_plane - 1 + n_high - 1 + 1
    if 1 in shared:
        expected = expected + jnp.where(present[1], 1, 0)

    def remote(src, dst, send, recv, device):
        return pltpu.make_async_remote_copy(
            src_ref=src, dst_ref=dst, send_sem=send, recv_sem=recv, device_id=device, device_id_type=MESH)

    def face_copy(r, f):
        return remote(sendb.at[r, f], recvb.at[r, landing[f]], face_send.at[r, f], face_recv.at[r, landing[f]], peer[f])

    def face_arrival(r, f):
        return remote(sendb.at[r, f], recvb.at[r, f], face_send.at[r, f], face_recv.at[r, f], peer[f])

    def basis_copy(f):
        return remote(b_out.at[f], b_in.at[landing[f]], n_send.at[0, f], n_recv.at[0, landing[f]], peer[f])

    def basis_arrival(f):
        return remote(b_out.at[f], b_in.at[f], n_send.at[0, f], n_recv.at[0, f], peer[f])

    def coarse_copy(c, f):
        return remote(x_out.at[c], x_in.at[c, landing[f]], n_send.at[1 + c, f], n_recv.at[1 + c, landing[f]], peer[f])

    def coarse_arrival(c, f):
        return remote(x_out.at[c], x_in.at[c, f], n_send.at[1 + c, f], n_recv.at[1 + c, f], peer[f])

    def modes_copy(k, slot):
        return remote(plane_modes.at[slot], plane_modes.at[slot], p_send.at[0, k], p_recv.at[0, k], plane_peer(k))

    def plane_copy(c, k, slot):
        return remote(plane.at[c, slot], plane.at[c, slot], p_send.at[1 + c, k], p_recv.at[1 + c, k], plane_peer(k))

    def from_plane(k):
        return lax.rem(mine + n_plane - k, n_plane)

    def line_copy(k, slot):
        return remote(line_out.at[line_at(k)], line_in.at[slot], z_send.at[0, k], z_recv.at[0, k], line_peer(k))

    def part_copy(c, k):
        return remote(part_out.at[c, line_at(k)], part_in.at[c, k], z_send.at[1 + c, k], z_recv.at[1 + c, k], line_peer(k))

    def from_line(k):
        return lax.rem(high + n_high - k, n_high)

    def send_face(r, f):
        if f in shared:
            guard(f, lambda: face_copy(r, f).start())

    def await_faces(r, slots):
        for f in [f for f in reversed(slots) if f in shared]:
            guard(f, lambda: face_arrival(r, f).wait_recv())

    def received(r, f):
        if f not in shared:
            return None
        value = recvb[r, f]
        return value if f in always else jnp.where(present[f], value, 0.0)

    def assembled(r, f):
        value = received(r, f)
        return sendb[r, f] if value is None else sendb[r, f] + value

    def halves(out):
        return out[:, :columns] + out[:, columns:]

    def put(ref, rows, value):
        upper, lower = split(value)
        ref[rows, :columns] = upper
        ref[rows, columns:] = lower

    def slot_rows(f):
        return slice(f * face, (f + 1) * face)

    map_row = fmap[...].astype(F32)
    map_column[...] = jnp.broadcast_to(map_row, (tile, order)).T
    lanes = lax.broadcasted_iota(jnp.int32, (face, tile), 1).astype(F32)
    for f in range(4):
        own = map_column[pl.ds(pl.multiple_of(face_of[f] * face, 16), face), :]
        for t in range(order // tile):
            perm[slot_rows(f), t * tile:(t + 1) * tile] = jnp.where(own == lanes + float(t * tile), 1.0, 0.0).astype(BF16)

    width = plane_modes.shape[2]
    row = lax.broadcasted_iota(jnp.int32, (modes, width), 0)
    lane = lax.broadcasted_iota(jnp.int32, (modes, width), 1)
    plane_modes[mine] = exact_dot(gm[...], jnp.where(lane == row + g * modes, 1.0, 0.0).astype(F32))
    own_modes = jnp.concatenate([gm[...], jnp.zeros((modes, tile - modes), F32)], axis=1)
    for h in range(n_high):
        line_out[h, :, :row_modes] = ginv[:, h * row_modes:(h + 1) * row_modes]
        line_out[h, :, row_modes:] = own_modes

    load_l.wait()
    for i in range(4):
        put(z2, slot_rows(i), stage_l[slot_rows(i), :])
    for f in late:
        sendb[0, f] = halves(dot(perm[slot_rows(f), :], z2[...]))
    pl.semaphore_wait(barrier, expected)
    for f in late:
        send_face(0, f)
    for f in (3, 2):
        sendb[0, f] = halves(dot(perm[slot_rows(f), :], z2[...]))
        send_face(0, f)

    for k in range(1, n_high):
        line_copy(k, high).start()
    for k in range(1, n_plane):
        modes_copy(k, mine).start()

    upper, lower = split(basis[...])
    both = jnp.concatenate([upper, lower], axis=0)
    for part in range(2):
        b2[part] = dot_last(both, perm[part * half:(part + 1) * half, :]).astype(BF16)
    for f in range(4):
        moved = dot_last(both, perm[slot_rows(f), :])
        b_out[f] = jnp.zeros(b_out.shape[1:], F32)
        b_out[f, :, :face] = moved[:modes] + moved[modes:]
        if f in shared:
            guard(f, lambda: basis_copy(f).start())

    def split_matrix(stage, matrix):
        def chunk(i, carry):
            rows = pl.ds(pl.multiple_of(i * tile, tile), tile)
            upper, lower = split(stage[rows, :])
            matrix[rows, :order] = upper
            matrix[rows, order:] = lower
            return carry
        lax.fori_loop(0, order // tile, chunk, 0)

    def permute_schur(start, stop):
        for i in range(start, stop):
            rows = slice(i // blocks * half, (i // blocks + 1) * half)
            lanes = slice(2 * (i % blocks) * tile, 2 * (i % blocks + 1) * tile)
            sp2[rows, lanes] = dot(perm[rows, :], s2[:, lanes]).astype(BF16)
    blocks = order // tile
    stages = [blocks // 2, blocks * 3 // 4, blocks * 4 // 3, 2 * blocks]
    held = 1 + len(shared)

    def own_bases():
        position = lax.broadcasted_iota(jnp.int32, (16, order), 1)
        weights = jnp.full((16, order), weight[0], F32)
        for f in range(1, 4):
            weights = jnp.where(position >= f * face, weight[f], weights)
        weights = dot(weights.astype(BF16), perm[...])[:1]
        for part in range(2):
            rows = slice(part * held * modes, (part * held + 1) * modes)
            gcat[rows, :] = (both[part * modes:(part + 1) * modes].astype(F32) * weights).astype(BF16)

    def neighbour_bases():
        for n, f in enumerate(shared):
            guard(f, lambda: basis_arrival(f).wait_recv())
            value = b_in[f] if f in always else jnp.where(present[f], b_in[f], 0.0)
            upper, lower = split(value * weight[f])
            moved = dot(jnp.concatenate([upper, lower], axis=0)[:, :face], perm[slot_rows(f), :])
            for part in range(2):
                base = (part * held + 1 + n) * modes
                gcat[base:base + modes, :] = moved[part * modes:(part + 1) * modes].astype(BF16)

    load_a.wait()
    split_matrix(stage_a, a2)
    load_s.wait()
    split_matrix(stage_s, s2)

    permute_schur(0, stages[0])

    third_rows = order // 3

    def thirds():
        for i in range(3):
            yield (slice(i * third_rows, (i + 1) * third_rows),
                   slice(order + i * third_rows, order + (i + 1) * third_rows))

    def begin():
        for rows, _ in thirds():
            early[rows, :] = dot_first(perm[half:, rows], x2[half:, :])

    def complete(rows):
        return early[rows, :] + dot_first(perm[:half, rows], x2[:half, :])

    def update_residual(r, weighted):
        for slots in (soon, late):
            await_faces(r, slots)
            for f in slots:
                value = assembled(r, f) if r == 0 else residual[f] - assembled(r, f)
                residual[f] = value
                put(x2, slot_rows(f), value * weight[f] if weighted else value)
            if slots is soon:
                begin()
                if weighted:
                    products[...] = dot(b2[1], x2[half:, :])

    update_residual(0, True)
    centre = jnp.full((1, columns), 0.5 * (spec[0] + spec[1]), F32)
    half_width = jnp.full((1, columns), 0.5 * (spec[1] - spec[0]), F32)

    def build_coarse():
        line_in[high] = line_out[high]
        for k in range(1, n_high):
            line_copy(k, from_line(k)).wait_recv()
        for k in range(1, n_plane):
            modes_copy(k, from_plane(k)).wait_recv()
        lines = line_in[...].reshape(n_high * modes, row_modes + tile)
        top_rows = top[pl.ds(pl.multiple_of(g * modes, modes), modes), :]
        through = exact_dot(lines[:, row_modes:row_modes + modes], top_rows)
        sources = plane_modes[...].reshape(n_plane * modes, width)[:, :n_grp * modes]
        for k in range(n_grp):
            part = lax.dot_general(
                through, sources[k * row_modes:(k + 1) * row_modes], LAST,
                precision=lax.Precision.HIGHEST, preferred_element_type=F32)
            part = part + jnp.where(g == k, lines[:, :row_modes], 0.0)
            upper, lower = split(part)
            t2[:n_high * modes, k * row_modes:(k + 1) * row_modes] = upper
            t2[n_high * modes:, k * row_modes:(k + 1) * row_modes] = lower

    def precondition(r, c, step, keep):
        block = halves(products[...] + dot(b2[0], x2[:half, :]))
        plane[c, mine] = block[:modes, :] + block[modes:, :]
        for k in range(1, n_plane):
            plane_copy(c, k, mine).start()
        for rows, second in thirds():
            out = complete(rows).astype(BF16)
            xl2[rows, :] = out
            xl2[second, :] = out
        for rows, _ in thirds():
            put(z2, rows, halves(dot(a2[rows, :], xl2[...])))

        def outward(slots):
            for f in slots:
                sendb[r, f] = halves(dot(perm[slot_rows(f), :], z2[...])) * weight[f]
                send_face(r, f)
        if c == 0:
            build_coarse()
        for k in range(1, n_plane):
            plane_copy(c, k, from_plane(k)).wait_recv()
        put(c2, slice(None), plane[c].reshape(n_plane * modes, columns))
        parts = halves(dot(t2[...], c2[...]))
        parts = parts[:n_high * modes] + parts[n_high * modes:]
        part_out[c] = parts.reshape(n_high, modes, columns)
        for k in range(1, n_high):
            part_copy(c, k).start()
        outward((0, 1, 3, 2))
        if c == 0:
            own_bases()
            neighbour_bases()
            permute_schur(stages[0], stages[1])
        await_faces(r, soon)
        for f in soon:
            put(x2, slot_rows(f), assembled(r, f))
        begin()
        update = part_out[c, high]
        for k in range(1, n_high):
            part_copy(c, k).wait_recv()
            update = update + part_in[c, k]
        x_out[c] = update
        for f in shared:
            guard(f, lambda: coarse_copy(c, f).start())
        if c == 0:
            permute_schur(stages[1], stages[2])

        def place(n, value):
            upper, lower = split(value)
            for base in (n * modes, (held + n) * modes):
                xcat[base:base + modes, :columns] = upper
                xcat[base:base + modes, columns:] = lower
        place(0, update)
        await_faces(r, late)
        for f in late:
            put(x2, slot_rows(f), assembled(r, f))
        for rows, _ in thirds():
            value = halves(complete(rows)) * step
            if keep is not None:
                value = value + direction[rows, :] * keep
            direction[rows, :] = value
        for f in reversed(shared):
            guard(f, lambda: coarse_arrival(c, f).wait_recv())
        for n, f in enumerate(shared):
            place(1 + n, x_in[c, f] if f in always else jnp.where(present[f], x_in[c, f], 0.0))
        for rows, second in thirds():
            value = direction[rows, :] + halves(dot_first(gcat[:, rows], xcat[...])) * step
            direction[rows, :] = value
            upper, lower = split(value)
            for part in (rows, second):
                xl2[part, :columns] = upper
                xl2[part, columns:] = lower

    precondition(1, 0, 1.0 / centre, None)
    rho = half_width / centre
    for turn in range(ITERS):
        r = 2 + 2 * turn
        for f in (0, 1, 3, 2):
            if turn == 0 and f == 3:
                permute_schur(stages[2], stages[3])
            sendb[r, f] = halves(dot(sp2[slot_rows(f), :], xl2[...]))
            send_face(r, f)
        total[...] = direction[...] if turn == 0 else total[...] + direction[...]
        if turn + 1 == ITERS:
            hand_total.start()
        update_residual(r, turn + 1 < ITERS)
        if turn + 1 < ITERS:
            rho_next = 1.0 / (2.0 * centre / half_width - rho)
            precondition(r + 1, 1 + turn, 2.0 * rho_next / half_width, rho_next * rho)
            rho = rho_next

    handed = []
    for i, (rows, _) in enumerate(thirds()):
        direction[rows, :] = halves(complete(rows))
        handed.append(pltpu.make_async_copy(direction.at[rows], res_out.at[rows], out_sem.at[1 + i]))
        handed[i].start()

    for r in range(1 + 2 * ITERS):
        for f in shared:
            guard(f, lambda: face_copy(r, f).wait_send())
    hand_total.wait()
    for copy in handed:
        copy.wait()
    for f in shared:
        guard(f, lambda: basis_copy(f).wait_send())
    for k in range(1, n_high):
        line_copy(k, high).wait_send()
    for k in range(1, n_plane):
        modes_copy(k, mine).wait_send()
    for c in range(ITERS):
        for k in range(1, n_plane):
            plane_copy(c, k, mine).wait_send()
        for k in range(1, n_high):
            part_copy(c, k).wait_send()
        for f in shared:
            guard(f, lambda: coarse_copy(c, f).wait_send())


def hand_out(sol, res, sol_out, res_out, held, arrive, leave):
    rows = held.shape[1] // 2
    steps = []
    for i in range(2):
        part = pl.ds(i * rows, rows)
        for n, (source, target) in enumerate(((sol, sol_out), (res, res_out))):
            steps.append((pltpu.make_async_copy(source.at[part], held.at[n, part], arrive.at[n, i]),
                          pltpu.make_async_copy(held.at[n, part], target.at[part], leave.at[n, i])))
    for first, _ in steps:
        first.start()
    for first, second in steps:
        first.wait()
        second.start()
    for _, second in steps:
        second.wait()


def solution(mesh):
    n_grp, n_sub = mesh.shape["grp"], mesh.shape["sub"]
    n_low = 1
    while n_low * n_low < n_sub:
        n_low *= 2
    n_high = n_sub // n_low
    n_plane = n_grp * n_low
    held = 3 + (1 if n_grp > 2 else 0) + (1 if n_sub > 2 else 0)

    def step(load, schur, linv, basis, ginv, gm, top, fmap, spec):
        order, columns = load.shape
        modes = basis.shape[0]
        face = order // 4
        padded = -(-face // 128) * 128
        width = -(-n_grp * modes // 128) * 128
        faces = 1 + 2 * ITERS
        vmem = pl.BlockSpec(memory_space=pltpu.VMEM)
        hbm = pl.BlockSpec(memory_space=pl.ANY)
        smem = pl.BlockSpec(memory_space=pltpu.SMEM)
        dma = pltpu.SemaphoreType.DMA
        field = jax.ShapeDtypeStruct((order, columns), F32)
        sol, res = pl.pallas_call(
            functools.partial(kernel, n_grp, n_sub, n_low),
            out_shape=(field, field),
            in_specs=[hbm, hbm, hbm, vmem, vmem, vmem, vmem, vmem, smem],
            out_specs=(hbm, hbm),
            scratch_shapes=[
                pltpu.VMEM((order, columns), F32),
                pltpu.VMEM((order, columns), F32),
                pltpu.VMEM((order, order), F32),
                pltpu.VMEM((order, order), F32),
                pltpu.VMEM((order, 2 * order), BF16),
                pltpu.VMEM((order, 2 * order), BF16),
                pltpu.VMEM((order, 2 * order), BF16),
                pltpu.VMEM((order, order), BF16),
                pltpu.VMEM((order, 128), F32),
                pltpu.VMEM((2, 2 * modes, 2 * face), BF16),
                pltpu.VMEM((2 * held * modes, order), BF16),
                pltpu.VMEM((order, 2 * columns), BF16),
                pltpu.VMEM((order, 2 * columns), F32),
                pltpu.VMEM((2 * modes, 2 * columns), F32),
                pltpu.VMEM((2 * order, 2 * columns), BF16),
                pltpu.VMEM((order, 2 * columns), BF16),
                pltpu.VMEM((2 * held * modes, 2 * columns), BF16),
                pltpu.VMEM((order, columns), F32),
                pltpu.VMEM((4, face, columns), F32),
                pltpu.VMEM((faces, 4, face, columns), F32),
                pltpu.VMEM((faces, 4, face, columns), F32),
                pltpu.VMEM((4, modes, padded), F32),
                pltpu.VMEM((4, modes, padded), F32),
                pltpu.VMEM((n_high, modes, n_low * modes + 128), F32),
                pltpu.VMEM((n_high, modes, n_low * modes + 128), F32),
                pltpu.VMEM((n_plane, modes, width), F32),
                pltpu.VMEM((2 * n_high * modes, n_plane * modes), BF16),
                pltpu.VMEM((ITERS, n_plane, modes, columns), F32),
                pltpu.VMEM((n_plane * modes, 2 * columns), BF16),
                pltpu.VMEM((ITERS, n_high, modes, columns), F32),
                pltpu.VMEM((ITERS, n_high, modes, columns), F32),
                pltpu.VMEM((ITERS, modes, columns), F32),
                pltpu.VMEM((ITERS, 4, modes, columns), F32),
                dma((3,)),
                dma((4,)),
                dma((faces, 4)),
                dma((faces, 4)),
                dma((1 + ITERS, n_plane)),
                dma((1 + ITERS, n_plane)),
                dma((1 + ITERS, n_high)),
                dma((1 + ITERS, n_high)),
                dma((1 + ITERS, 4)),
                dma((1 + ITERS, 4)),
            ],
            compiler_params=pltpu.CompilerParams(
                collective_id=0, has_side_effects=True, vmem_limit_bytes=60 * 1024 * 1024
            ),
        )(load, schur, linv, basis, ginv, gm, top, fmap, spec)
        return pl.pallas_call(
            hand_out, out_shape=(field, field), in_specs=[hbm, hbm], out_specs=(hbm, hbm),
            scratch_shapes=[pltpu.VMEM((2, order, columns), F32), dma((2, 2)), dma((2, 2))],
        )(sol, res)

    row = P(("grp", "sub"), None)
    return jax.shard_map(
        step,
        mesh=mesh,
        in_specs=(row, row, row, row, row, row, P(), row, P()),
        out_specs=(row, row),
        check_vma=False,
    )
```
